32 devices in a mesh: col: 32 (over z, y, x, core).
Axes of the slice: x: 2, y: 2, z: 4, core: 2. Of those that a mesh axis runs over, the one named last changes fastest.
Arguments:
- covariance: float32 [2, 8192, 8192], P(None, 'col'), may hold values from -6 to 6, as said below
- forcing: float32 [2, 8192, 8192], P(None, 'col'), may hold values from -24 to 24, as said below
- coefficient: float32 [2, 64, 128], replicated, may hold values from 0.5 to 1.5
- y_operator: float32 [2, 64, 64], replicated, may hold values from -0.75 to 0.75
- z_operator: float32 [2, 128, 128], replicated, may hold values from -0.5 to 0.5
Outputs:
- advanced: float32 [2, 8192, 8192], P(None, 'col')
The draws below stay inside these ranges and needn't reach their ends.
Inputs may be any that keep to these rules, and one draw needn't show every extreme that they name: Each harmonic's covariance is symmetric. Each harmonic's forcing is symmetric.
All inputs are finite; a program needn't handle non-finite values.
Results may differ from the reference program's by a relative error of at most 0.0001.
Values sent between devices are 32-bit elements; how exact they have to be, the bound alone decides.
No kernel may reach another device: no remote copies, remote signals or barrier semaphores. Data moves between devices by JAX's collectives and lax.ppermute only.
A program may use at most 256 MiB of HBM per device.

```python
import jax
import jax.numpy as jnp
from jax import lax

NY = 64
NZ = 128
N = 8192


def symmetric_draw(key, scale):
    raw = jax.random.normal(key, (2, N, N), jnp.float32)
    sym = jnp.clip((raw + jnp.swapaxes(raw, 1, 2)) * 0.70710678, -6.0, 6.0)
    return scale * sym


def draw_covariance(key, part):
    return symmetric_draw(jax.random.fold_in(key, 11), 1.0)


def draw_forcing(key, part):
    return symmetric_draw(jax.random.fold_in(key, 23), 4.0)


def gaussian(rng, shape, spread, most, kind=jnp.bfloat16):
    drawn = spread * jax.random.normal(rng, shape, jnp.float32)
    return jnp.clip(drawn, min=-most, max=most).astype(kind)


def setup_inputs(seed: int = 0) -> dict:
    splits = jax.random.split(jax.random.key(seed), 6)
    covariance = draw_covariance(jax.random.fold_in(splits[5], 71), 0)
    forcing = draw_forcing(jax.random.fold_in(splits[5], 71), 0)
    coefficient = jnp.clip(jax.random.uniform(splits[2], (2, NY, NZ), jnp.float32, 0.5, 1.5), 0.5, 1.5)
    y_operator = gaussian(splits[3], (2, NY, NY), NY ** -0.5, 0.75, jnp.float32)
    z_operator = gaussian(splits[4], (2, NZ, NZ), NZ ** -0.5, 0.5, jnp.float32)
    return {"covariance": covariance, "forcing": forcing, "coefficient": coefficient, "y_operator": y_operator, "z_operator": z_operator}


step_size = 0.2


def combined(values, y_matrix, z_matrix):
    along_y = jnp.einsum("ya,azc->yzc", y_matrix, values, precision=lax.Precision.HIGHEST)
    along_z = jnp.einsum("zb,ybc->yzc", z_matrix, values, precision=lax.Precision.HIGHEST)
    return along_y + along_z


def apply_operator(columns, y_matrix, z_matrix, gain_field):
    grid = columns.reshape(NY, NZ, -1)
    inner = gain_field[:, :, None] * combined(grid, y_matrix, z_matrix)
    return combined(inner, y_matrix, z_matrix).reshape(NY * NZ, -1)


def slope_of(state, y_matrix, z_matrix, gain_field, source):
    product = apply_operator(state, y_matrix, z_matrix, gain_field)
    return product + product.T + source


def reference(covariance, forcing, coefficient, y_operator, z_operator):
    results = []
    for harmonic in range(2):
        start = covariance[harmonic]
        args = (y_operator[harmonic], z_operator[harmonic], coefficient[harmonic], forcing[harmonic])
        slope_one = slope_of(start, *args)
        slope_two = slope_of(start + (0.5 * step_size) * slope_one, *args)
        slope_three = slope_of(start + (0.5 * step_size) * slope_two, *args)
        slope_four = slope_of(start + step_size * slope_three, *args)
        results.append(start + (step_size / 6.0) * (slope_one + 2.0 * slope_two + 2.0 * slope_three + slope_four))
    return jnp.stack(results)
```

```python
import functools

import jax
import jax.numpy as jnp
from jax import lax
from jax.experimental import pallas as pl
from jax.experimental.pallas import tpu as pltpu
from jax.sharding import PartitionSpec as P

step_size = 0.2
lanes = 128
sublanes = 8
tiles = 4
group = 8


def split(value):
    high = value.astype(jnp.bfloat16)
    low = (value - high.astype(jnp.float32)).astype(jnp.bfloat16)
    return high, low


def operator_pair(value):
    high = lax.reduce_precision(value, exponent_bits=8, mantissa_bits=7)
    return high.astype(jnp.bfloat16), (value - high).astype(jnp.bfloat16)


def combined(rows, y_pair, z_pair):
    grid_y = rows[0].shape[0]
    pairs = [split(row) for row in rows]
    right = jnp.concatenate([jnp.concatenate(pair, axis=0) for pair in pairs], axis=1)
    left = jnp.concatenate([jnp.concatenate(pair, axis=1) for pair in pairs], axis=0)
    along_y = jnp.dot(y_pair, right, preferred_element_type=jnp.float32)
    along_z = jnp.dot(left, z_pair, preferred_element_type=jnp.float32)
    out = []
    for i in range(len(rows)):
        y_part = along_y[:, i * lanes : (i + 1) * lanes]
        z_part = along_z[i * grid_y : (i + 1) * grid_y]
        out.append(
            (y_part[:grid_y] + y_part[grid_y:]) + (z_part[:, :lanes] + z_part[:, lanes:])
        )
    return out


def operate(rows, y_pair, z_pair, gain):
    inner = [gain * row for row in combined(rows, y_pair, z_pair)]
    return combined(inner, y_pair, z_pair)


def body(stage, grid_y, *refs):
    y_ref, z_ref, gain_ref, *ins = refs[: 3 + {"first": 1, "second": 3, "third": 4}[stage]]
    outs = refs[3 + len(ins) :]
    result_ref, sent_ref = outs[0], outs[1]
    inner = pl.program_id(1)
    y_pair, z_pair, gain = y_ref[0], z_ref[0], gain_ref[0]

    def tiled(ref, t, r):
        return ref[0, t, pl.ds(r, grid_y, stride=sublanes), :]

    def arrived(ref, t, r):
        flat = ref.reshape(grid_y * tiles * sublanes, lanes)
        return flat[pl.ds(t * sublanes + r, grid_y, stride=tiles * sublanes), :]

    def per_tile(t, carry):
        for r0 in range(0, sublanes, group):
            each = range(r0, r0 + group)
            if stage == "first":
                (state,) = ins
                out = operate([tiled(state, t, r) for r in each], y_pair, z_pair, gain)
            elif stage == "second":
                product, crossed, forcing = ins
                slopes = [
                    tiled(product, t, r) + arrived(crossed, t, r) + step_size * tiled(forcing, t, r)
                    for r in each
                ]
                for r, slope in zip(each, slopes):
                    outs[2][0, t, r] = slope
                out = operate(slopes, y_pair, z_pair, gain)
            else:
                product, crossed, slope, state = ins
                firsts = [
                    slope[0, t, r] * (1 / 6)
                    + arrived(crossed, t, r) * 0.125
                    + tiled(product, t, r) * (1 / 24)
                    for r in each
                ]
                seconds = [
                    slope[0, t, r] * 0.5 + arrived(crossed, t, r) * (1 / 6) + value
                    for r, value in zip(each, operate(firsts, y_pair, z_pair, gain))
                ]
                out = [
                    0.5 * (slope[0, t, r] + tiled(state, t, r)) + value
                    for r, value in zip(each, operate(seconds, y_pair, z_pair, gain))
                ]
            for r, value in zip(each, out):
                result_ref[0, inner * tiles + t, pl.ds(r, grid_y, stride=sublanes), :] = value
        return carry

    lax.fori_loop(0, tiles, per_tile, 0)

    @pl.when(inner == pl.num_programs(1) - 1)
    def _():
        owners, _, columns = sent_ref.shape[:3]

        def per_owner(d, carry):
            for c in range(columns):
                start = pl.multiple_of((d * columns + c) * sublanes, sublanes)
                block = result_ref[0, :, pl.ds(start, sublanes), :].reshape(lanes, lanes)
                sent_ref[d, 0, c] = block.T
            return carry

        lax.fori_loop(0, owners, per_owner, 0)


def stage_call(stage, harmonic, groups, grid_y, width, y_pair, z_pair, gain, *operands):
    chunk = tiles * sublanes
    inner = lanes // chunk
    per = width // lanes
    row_tiles = width // sublanes
    rows = grid_y * sublanes

    def whole(shape):
        return pl.BlockSpec((1, *shape), lambda k, i: (harmonic, 0, 0))

    def tile_spec(which):
        return pl.BlockSpec((1, tiles, rows, lanes), lambda k, i: (which, k * inner + i, 0, 0))

    crossed = pl.BlockSpec((grid_y, chunk, lanes), lambda k, i: (0, k * inner + i, 0))
    slope = pl.BlockSpec(
        (1, tiles, sublanes, grid_y, lanes), lambda k, i: (0, k * inner + i, 0, 0, 0)
    )
    ins = {
        "first": [tile_spec(harmonic)],
        "second": [tile_spec(0), crossed, tile_spec(harmonic)],
        "third": [tile_spec(0), crossed, slope, tile_spec(harmonic)],
    }[stage]
    out_specs = [
        pl.BlockSpec((1, lanes // sublanes, rows, lanes), lambda k, i: (0, k, 0, 0)),
        pl.BlockSpec((groups, 1, per, lanes, lanes), lambda k, i: (0, k, 0, 0, 0)),
    ]
    out_shape = [
        jax.ShapeDtypeStruct((1, row_tiles, rows, lanes), jnp.float32),
        jax.ShapeDtypeStruct((groups, per, per, lanes, lanes), jnp.float32),
    ]
    if stage == "second":
        out_specs.append(slope)
        out_shape.append(
            jax.ShapeDtypeStruct((1, row_tiles, sublanes, grid_y, lanes), jnp.float32)
        )
    passes = 2 if stage == "third" else 1
    return pl.pallas_call(
        functools.partial(body, stage, grid_y),
        grid=(per, inner),
        in_specs=[
            whole((2 * grid_y, 2 * grid_y)),
            whole((2 * lanes, 2 * lanes)),
            whole((grid_y, lanes)),
            *ins,
        ],
        out_specs=out_specs,
        out_shape=out_shape,
        cost_estimate=pl.CostEstimate(
            flops=passes * 16 * width * grid_y * lanes * (grid_y + lanes),
            bytes_accessed=(len(ins) + len(out_specs)) * width * grid_y * lanes * 4,
            transcendentals=0,
        ),
        compiler_params=pltpu.CompilerParams(vmem_limit_bytes=60 * 1024 * 1024),
        name=f"{stage}_{harmonic}",
    )(y_pair, z_pair, gain, *operands)


def finish_body(per_step, *refs):
    product_ref, crossed_ref, out_ref = refs[0], refs[1], refs[-1]
    for j in range(per_step):
        half = product_ref[0, :, j * sublanes : (j + 1) * sublanes, :]
        out_ref[0, :, j * lanes : (j + 1) * lanes] = half.reshape(-1, lanes) + crossed_ref[j]


def finish_call(harmonic, product, crossed, out):
    grid_y, width, _ = crossed.shape
    per_step = 8 if grid_y % 8 == 0 else 1
    row_tiles = width // sublanes
    in_specs = [
        pl.BlockSpec((1, row_tiles, per_step * sublanes, lanes), lambda i: (0, 0, i, 0)),
        pl.BlockSpec((per_step, width, lanes), lambda i: (i, 0, 0)),
    ]
    operands = [product, crossed]
    aliases = {}
    if out is not None:
        in_specs.append(pl.BlockSpec(memory_space=pl.ANY))
        operands.append(out)
        aliases = {2: 0}
    return pl.pallas_call(
        functools.partial(finish_body, per_step),
        grid=(grid_y // per_step,),
        in_specs=in_specs,
        out_specs=pl.BlockSpec((1, width, per_step * lanes), lambda i: (harmonic, 0, i)),
        out_shape=jax.ShapeDtypeStruct((2, width, grid_y * lanes), jnp.float32),
        input_output_aliases=aliases,
        cost_estimate=pl.CostEstimate(
            flops=width * grid_y * lanes,
            bytes_accessed=3 * width * grid_y * lanes * 4,
            transcendentals=0,
        ),
        compiler_params=pltpu.CompilerParams(vmem_limit_bytes=48 * 1024 * 1024),
        name=f"finish_{harmonic}",
    )(*operands)


def exchange(sent):
    received = lax.all_to_all(sent, "col", split_axis=0, concat_axis=0, tiled=True)
    groups, per = sent.shape[:2]
    return received.reshape(groups * per, per * lanes, lanes)


def on_device_tiled(covariance, forcing, coefficient, y_operator, z_operator):
    groups = lax.axis_size("col")
    width = covariance.shape[1]
    grid_y = y_operator.shape[1]

    def by_tiles(value):
        cut = value.reshape(2, width // sublanes, sublanes, grid_y, lanes)
        return jnp.swapaxes(cut, 2, 3).reshape(2, width // sublanes, grid_y * sublanes, lanes)

    y_high, y_low = operator_pair(y_operator)
    z_high, z_low = operator_pair(jnp.swapaxes(z_operator, 1, 2))
    y_pair = jnp.concatenate(
        [jnp.concatenate([y_high, y_high], axis=2), jnp.concatenate([y_low, y_low], axis=2)], axis=1
    )
    z_pair = jnp.concatenate([jnp.concatenate([z_high, z_low], axis=2)] * 2, axis=1)
    gain = step_size * coefficient
    state, source = by_tiles(covariance), by_tiles(forcing)

    def call(stage, harmonic, *operands):
        return stage_call(
            stage, harmonic, groups, grid_y, width, y_pair, z_pair, gain, *operands
        )

    first = [call("first", h, state) for h in range(2)]
    crossed = [exchange(sent) for _, sent in first]
    second = [call("second", h, first[h][0], crossed[h], source) for h in range(2)]
    crossed = [exchange(sent) for _, sent, _ in second]
    third = [call("third", h, second[h][0], crossed[h], second[h][2], state) for h in range(2)]
    crossed = [exchange(sent) for _, sent in third]
    out = None
    for h in range(2):
        out = finish_call(h, third[h][0], crossed[h], out)
    return out


def on_device_plain(covariance, forcing, coefficient, y_operator, z_operator):
    grid_y, grid_z = y_operator.shape[1], z_operator.shape[1]
    width = covariance.shape[1]
    groups = lax.axis_size("col")

    def along(values):
        part = jnp.einsum("hya,hcaz->hcyz", y_operator, values, precision=lax.Precision.HIGHEST)
        other = jnp.einsum("hcyb,hzb->hcyz", values, z_operator, precision=lax.Precision.HIGHEST)
        return part + other

    def operated(slab):
        grid = slab.reshape(2, width, grid_y, grid_z)
        return along(step_size * coefficient[:, None] * along(grid)).reshape(slab.shape)

    def crossed(product):
        received = lax.all_to_all(product, "col", split_axis=2, concat_axis=2, tiled=True)
        blocks = received.reshape(2, width, groups, width)
        return jnp.swapaxes(blocks, 1, 3).reshape(2, width, groups * width)

    product = operated(covariance)
    slope = product + crossed(product) + step_size * forcing
    product = operated(slope)
    other = crossed(product)
    inner = slope / 2 + other / 6 + operated(slope / 6 + other / 8 + product / 24)
    half = (covariance + slope) / 2 + operated(inner)
    return half + crossed(half)


def on_device(covariance, forcing, coefficient, y_operator, z_operator):
    width = covariance.shape[1]
    grid_y, grid_z = y_operator.shape[1], z_operator.shape[1]
    tiled = grid_z == lanes and width % lanes == 0 and grid_y % 16 == 0
    chosen = on_device_tiled if tiled else on_device_plain
    return chosen(covariance, forcing, coefficient, y_operator, z_operator)


def solution(mesh):
    placed = (P(None, "col", None), P(None, "col", None), P(), P(), P())
    return jax.shard_map(
        on_device, mesh=mesh, in_specs=placed, out_specs=P(None, "col", None), check_vma=False
    )
```

```python
import functools

import jax
import jax.numpy as jnp
from jax import lax
from jax.experimental import pallas as pl
from jax.experimental.pallas import tpu as pltpu
from jax.sharding import PartitionSpec as P

step_size = 0.2
lanes = 128
sublanes = 8
tiles = 4
group = 8


def split(value):
    high = value.astype(jnp.bfloat16)
    low = (value - high.astype(jnp.float32)).astype(jnp.bfloat16)
    return high, low


def combined(rows, y_pair, z_pair):
    grid_y = rows[0].shape[0]
    pairs = [split(row) for row in rows]
    right = jnp.concatenate([jnp.concatenate(pair, axis=0) for pair in pairs], axis=1)
    left = jnp.concatenate([jnp.concatenate(pair, axis=1) for pair in pairs], axis=0)
    along_y = jnp.dot(y_pair, right, preferred_element_type=jnp.float32)
    along_z = jnp.dot(left, z_pair, preferred_element_type=jnp.float32)
    out = []
    for i in range(len(rows)):
        y_part = along_y[:, i * lanes : (i + 1) * lanes]
        z_part = along_z[i * grid_y : (i + 1) * grid_y]
        out.append(
            (y_part[:grid_y] + y_part[grid_y:]) + (z_part[:, :lanes] + z_part[:, lanes:])
        )
    return out


def operate(rows, y_pair, z_pair, gain):
    inner = [gain * row for row in combined(rows, y_pair, z_pair)]
    return combined(inner, y_pair, z_pair)


def prepare(y_ref, z_ref, y_pair_ref, z_pair_ref):
    grid_y = y_ref.shape[1]
    for part, value in enumerate(split(y_ref[0])):
        for side in range(2):
            y_pair_ref[pl.ds(part * grid_y, grid_y), pl.ds(side * grid_y, grid_y)] = value
    for part, value in enumerate(split(z_ref[0].T)):
        for side in range(2):
            z_pair_ref[pl.ds(side * lanes, lanes), pl.ds(part * lanes, lanes)] = value


def body(stage, grid_y, *refs):
    y_ref, z_ref, gain_ref, *refs = refs
    *refs, y_pair_ref, z_pair_ref = refs
    half, inner = pl.program_id(0), pl.program_id(1)
    chunk = tiles * sublanes

    @pl.when((half == 0) & (inner == 0))
    def _():
        prepare(y_ref, z_ref, y_pair_ref, z_pair_ref)

    if stage == "first":
        state, sent_ref = refs
    elif stage == "second":
        crossed, product, forcing, result_ref, sent_ref, slope_ref, turned_ref = refs
        owners, per = crossed.shape[:2]

        @pl.when(inner == 0)
        def _():
            def per_source(s, carry):
                for k in range(per):
                    turned_ref[s * per + k] = crossed[s, k, 0].T
                return carry

            lax.fori_loop(0, owners, per_source, 0)

    else:
        crossed, product, slope, state, result_ref, sent_ref = refs
    y_pair, z_pair, gain = y_pair_ref[...], z_pair_ref[...], step_size * gain_ref[0]

    def tiled(ref, t, r):
        return ref[0, t, pl.ds(r, grid_y, stride=sublanes), :]

    def across(ref, row):
        rows = ref.shape[-2]
        return ref.reshape(grid_y * rows, lanes)[pl.ds(row, grid_y, stride=rows), :]

    def per_tile(t, carry):
        for r0 in range(0, sublanes, group):
            each = range(r0, r0 + group)
            if stage == "first":
                out = operate([tiled(state, t, r) for r in each], y_pair, z_pair, gain)
                flat = sent_ref.reshape(grid_y * chunk, lanes)
                for r, value in zip(each, out):
                    flat[pl.ds(t * sublanes + r, grid_y, stride=chunk), :] = value
                continue
            if stage == "second":
                slopes = [
                    across(product, t * sublanes + r)
                    + across(turned_ref, inner * chunk + t * sublanes + r)
                    + step_size * tiled(forcing, t, r)
                    for r in each
                ]
                for r, value in zip(each, slopes):
                    slope_ref[0, t, r] = value
                out = operate(slopes, y_pair, z_pair, gain)
            else:
                arrived = [across(crossed, t * sublanes + r) for r in each]
                firsts = [
                    slope[0, t, r] * (1 / 6) + value * 0.125 + tiled(product, t, r) * (1 / 24)
                    for r, value in zip(each, arrived)
                ]
                seconds = [
                    slope[0, t, r] * 0.5 + across(crossed, t * sublanes + r) * (1 / 6) + value
                    for r, value in zip(each, operate(firsts, y_pair, z_pair, gain))
                ]
                out = [
                    0.5 * (slope[0, t, r] + tiled(state, t, r)) + value
                    for r, value in zip(each, operate(seconds, y_pair, z_pair, gain))
                ]
            for r, value in zip(each, out):
                result_ref[0, inner * tiles + t, pl.ds(r, grid_y, stride=sublanes), :] = value
        return carry

    lax.fori_loop(0, tiles, per_tile, 0, unroll=tiles if stage == "first" else 1)
    if stage == "first":
        return

    @pl.when(inner == pl.num_programs(1) - 1)
    def _():
        owners, _, columns = sent_ref.shape[:3]

        def per_owner(d, carry):
            for c in range(columns):
                start = pl.multiple_of((d * columns + c) * sublanes, sublanes)
                block = result_ref[0, :, pl.ds(start, sublanes), :].reshape(lanes, lanes)
                sent_ref[d, 0, c] = block.T
            return carry

        lax.fori_loop(0, owners, per_owner, 0)


def stage_call(stage, harmonic, groups, grid_y, width, y_operator, z_operator, gain, *operands):
    chunk = tiles * sublanes
    inner = lanes // chunk
    per = width // lanes
    row_tiles = width // sublanes
    rows = grid_y * sublanes

    def whole(shape):
        return pl.BlockSpec((1, *shape), lambda k, i: (harmonic, 0, 0))

    def tile_spec(which):
        return pl.BlockSpec((1, tiles, rows, lanes), lambda k, i: (which, k * inner + i, 0, 0))

    by_rows = pl.BlockSpec((groups, 1, per, chunk, lanes), lambda k, i: (0, k, 0, i, 0))
    unturned = pl.BlockSpec((groups, per, 1, lanes, lanes), lambda k, i: (0, 0, k, 0, 0))
    turned = pl.BlockSpec((grid_y, chunk, lanes), lambda k, i: (0, k * inner + i, 0))
    slope = pl.BlockSpec(
        (1, tiles, sublanes, grid_y, lanes), lambda k, i: (0, k * inner + i, 0, 0, 0)
    )
    ins = {
        "first": [tile_spec(harmonic)],
        "second": [unturned, by_rows, tile_spec(harmonic)],
        "third": [turned, tile_spec(0), slope, tile_spec(harmonic)],
    }[stage]
    blocks = jax.ShapeDtypeStruct((groups, per, per, lanes, lanes), jnp.float32)
    if stage == "first":
        out_specs, out_shape = [by_rows], [blocks]
    else:
        out_specs = [
            pl.BlockSpec((1, lanes // sublanes, rows, lanes), lambda k, i: (0, k, 0, 0)),
            pl.BlockSpec((groups, 1, per, lanes, lanes), lambda k, i: (0, k, 0, 0, 0)),
        ]
        out_shape = [jax.ShapeDtypeStruct((1, row_tiles, rows, lanes), jnp.float32), blocks]
    scratch = [
        pltpu.VMEM((2 * grid_y, 2 * grid_y), jnp.bfloat16),
        pltpu.VMEM((2 * lanes, 2 * lanes), jnp.bfloat16),
    ]
    if stage == "second":
        out_specs.append(slope)
        out_shape.append(
            jax.ShapeDtypeStruct((1, row_tiles, sublanes, grid_y, lanes), jnp.float32)
        )
        scratch.insert(0, pltpu.VMEM((grid_y, lanes, lanes), jnp.float32))
    passes = 2 if stage == "third" else 1
    return pl.pallas_call(
        functools.partial(body, stage, grid_y),
        grid=(per, inner),
        in_specs=[
            whole((grid_y, grid_y)),
            whole((lanes, lanes)),
            whole((grid_y, lanes)),
            *ins,
        ],
        out_specs=out_specs,
        out_shape=out_shape,
        scratch_shapes=scratch,
        cost_estimate=pl.CostEstimate(
            flops=passes * 16 * width * grid_y * lanes * (grid_y + lanes),
            bytes_accessed=(len(ins) + len(out_specs)) * width * grid_y * lanes * 4,
            transcendentals=0,
        ),
        compiler_params=pltpu.CompilerParams(vmem_limit_bytes=60 * 1024 * 1024),
        name=f"{stage}_{harmonic}",
    )(y_operator, z_operator, gain, *operands)


def finish_body(per_step, *refs):
    product_ref, crossed_ref, out_ref = refs[0], refs[1], refs[-1]
    for j in range(per_step):
        half = product_ref[0, :, j * sublanes : (j + 1) * sublanes, :]
        out_ref[0, :, j * lanes : (j + 1) * lanes] = half.reshape(-1, lanes) + crossed_ref[j]


def finish_call(harmonic, product, crossed, out):
    grid_y, width, _ = crossed.shape
    per_step = 8 if grid_y % 8 == 0 else 1
    row_tiles = width // sublanes
    in_specs = [
        pl.BlockSpec((1, row_tiles, per_step * sublanes, lanes), lambda i: (0, 0, i, 0)),
        pl.BlockSpec((per_step, width, lanes), lambda i: (i, 0, 0)),
    ]
    operands = [product, crossed]
    aliases = {}
    if out is not None:
        in_specs.append(pl.BlockSpec(memory_space=pl.ANY))
        operands.append(out)
        aliases = {2: 0}
    return pl.pallas_call(
        functools.partial(finish_body, per_step),
        grid=(grid_y // per_step,),
        in_specs=in_specs,
        out_specs=pl.BlockSpec((1, width, per_step * lanes), lambda i: (harmonic, 0, i)),
        out_shape=jax.ShapeDtypeStruct((2, width, grid_y * lanes), jnp.float32),
        input_output_aliases=aliases,
        cost_estimate=pl.CostEstimate(
            flops=width * grid_y * lanes,
            bytes_accessed=3 * width * grid_y * lanes * 4,
            transcendentals=0,
        ),
        compiler_params=pltpu.CompilerParams(vmem_limit_bytes=48 * 1024 * 1024),
        name=f"finish_{harmonic}",
    )(*operands)


def exchange(sent):
    return lax.all_to_all(sent, "col", split_axis=0, concat_axis=0, tiled=True)


def on_device_tiled(covariance, forcing, coefficient, y_operator, z_operator):
    groups = lax.axis_size("col")
    width = covariance.shape[1]
    per = width // lanes
    grid_y = y_operator.shape[1]

    def by_tiles(value):
        cut = value.reshape(2, width // sublanes, sublanes, grid_y, lanes)
        return jnp.swapaxes(cut, 2, 3).reshape(2, width // sublanes, grid_y * sublanes, lanes)

    def by_y(blocks):
        return blocks.reshape(groups * per, per * lanes, lanes)

    state, source = by_tiles(covariance), by_tiles(forcing)

    def call(stage, harmonic, *operands):
        return stage_call(
            stage, harmonic, groups, grid_y, width, y_operator, z_operator, coefficient, *operands
        )

    first = [call("first", h, state)[0] for h in range(2)]
    crossed = [exchange(sent) for sent in first]
    second = [call("second", h, crossed[h], first[h], source) for h in range(2)]
    crossed = [by_y(exchange(sent)) for _, sent, _ in second]
    third = [call("third", h, crossed[h], second[h][0], second[h][2], state) for h in range(2)]
    crossed = [by_y(exchange(sent)) for _, sent in third]
    out = None
    for h in range(2):
        out = finish_call(h, third[h][0], crossed[h], out)
    return out


def on_device_plain(covariance, forcing, coefficient, y_operator, z_operator):
    grid_y, grid_z = y_operator.shape[1], z_operator.shape[1]
    width = covariance.shape[1]
    groups = lax.axis_size("col")

    def along(values):
        part = jnp.einsum("hya,hcaz->hcyz", y_operator, values, precision=lax.Precision.HIGHEST)
        other = jnp.einsum("hcyb,hzb->hcyz", values, z_operator, precision=lax.Precision.HIGHEST)
        return part + other

    def operated(slab):
        grid = slab.reshape(2, width, grid_y, grid_z)
        return along(step_size * coefficient[:, None] * along(grid)).reshape(slab.shape)

    def crossed(product):
        received = lax.all_to_all(product, "col", split_axis=2, concat_axis=2, tiled=True)
        blocks = received.reshape(2, width, groups, width)
        return jnp.swapaxes(blocks, 1, 3).reshape(2, width, groups * width)

    product = operated(covariance)
    slope = product + crossed(product) + step_size * forcing
    product = operated(slope)
    other = crossed(product)
    inner = slope / 2 + other / 6 + operated(slope / 6 + other / 8 + product / 24)
    half = (covariance + slope) / 2 + operated(inner)
    return half + crossed(half)


def on_device(covariance, forcing, coefficient, y_operator, z_operator):
    width = covariance.shape[1]
    grid_y, grid_z = y_operator.shape[1], z_operator.shape[1]
    tiled = grid_z == lanes and width % lanes == 0 and grid_y % 16 == 0
    chosen = on_device_tiled if tiled else on_device_plain
    return chosen(covariance, forcing, coefficient, y_operator, z_operator)


def solution(mesh):
    placed = (P(None, "col", None), P(None, "col", None), P(), P(), P())
    return jax.shard_map(
        on_device, mesh=mesh, in_specs=placed, out_specs=P(None, "col", None), check_vma=False
    )
```

```python
import functools

import jax
import jax.numpy as jnp
from jax import lax
from jax.experimental import pallas as pl
from jax.experimental.pallas import tpu as pltpu
from jax.sharding import PartitionSpec as P

step_size = 0.2
lanes = 128
sublanes = 8
tiles = 4
group = sublanes


def split(value):
    high = value.astype(jnp.bfloat16)
    low = (value - high.astype(jnp.float32)).astype(jnp.bfloat16)
    return high, low


def combined(rows, y_pair, z_pair):
    grid_y = rows[0].shape[0]
    pairs = [split(row) for row in rows]
    right = jnp.concatenate([jnp.concatenate(pair, axis=0) for pair in pairs], axis=1)
    left = jnp.concatenate([jnp.concatenate(pair, axis=1) for pair in pairs], axis=0)
    along_y = jnp.dot(y_pair, right, preferred_element_type=jnp.float32)
    along_z = jnp.dot(left, z_pair, preferred_element_type=jnp.float32)
    out = []
    for i in range(len(rows)):
        y_part = along_y[:, i * lanes : (i + 1) * lanes]
        z_part = along_z[i * grid_y : (i + 1) * grid_y]
        out.append(
            (y_part[:grid_y] + y_part[grid_y:]) + (z_part[:, :lanes] + z_part[:, lanes:])
        )
    return out


def operate(rows, y_pair, z_pair, gain):
    inner = [gain * row for row in combined(rows, y_pair, z_pair)]
    return combined(inner, y_pair, z_pair)


def prepare(y_ref, z_ref, y_pair_ref, z_pair_ref):
    grid_y = y_ref.shape[1]
    for part, value in enumerate(split(y_ref[0])):
        for side in range(2):
            y_pair_ref[pl.ds(part * grid_y, grid_y), pl.ds(side * grid_y, grid_y)] = value
    for part, value in enumerate(split(z_ref[0].T)):
        for side in range(2):
            z_pair_ref[pl.ds(side * lanes, lanes), pl.ds(part * lanes, lanes)] = value


def body(stage, grid_y, *refs):
    y_ref, z_ref, gain_ref, *refs = refs
    *refs, y_pair_ref, z_pair_ref = refs
    half, inner = pl.program_id(0), pl.program_id(1)
    chunk = tiles * sublanes

    @pl.when((half == 0) & (inner == 0))
    def _():
        prepare(y_ref, z_ref, y_pair_ref, z_pair_ref)

    if stage == "first":
        state, sent_ref, tile_ref = refs
    elif stage == "second":
        crossed, product, forcing, result_ref, sent_ref, slope_ref, turned_ref = refs
        owners, per = crossed.shape[:2]

        @pl.when(inner == 0)
        def _():
            def per_source(s, carry):
                for k in range(per):
                    turned_ref[s * per + k] = crossed[s, k, 0].T
                return carry

            lax.fori_loop(0, owners, per_source, 0)

    else:
        crossed, product, slope, state, result_ref, sent_ref = refs
    y_pair, z_pair, gain = y_pair_ref[...], z_pair_ref[...], step_size * gain_ref[0]

    def tiled(ref, t, r):
        return ref[0, t, pl.ds(r, grid_y, stride=sublanes), :]

    def across(ref, row):
        rows = ref.shape[-2]
        return ref.reshape(grid_y * rows, lanes)[pl.ds(row, grid_y, stride=rows), :]

    def per_tile(t, carry):
        for r0 in range(0, sublanes, group):
            each = range(r0, r0 + group)
            if stage == "first":
                out = operate([tiled(state, t, r) for r in each], y_pair, z_pair, gain)
                flat = sent_ref.reshape(grid_y * chunk, lanes)
                for r, value in zip(each, out):
                    tile_ref[t, pl.ds(r, grid_y, stride=sublanes), :] = value
                for y in range(grid_y):
                    start = pl.multiple_of(y * chunk + t * sublanes, sublanes)
                    flat[pl.ds(start, sublanes), :] = tile_ref[t, pl.ds(y * sublanes, sublanes), :]
                continue
            if stage == "second":
                slopes = [
                    across(product, t * sublanes + r)
                    + across(turned_ref, inner * chunk + t * sublanes + r)
                    + step_size * tiled(forcing, t, r)
                    for r in each
                ]
                for r, value in zip(each, slopes):
                    slope_ref[0, t, r] = value
                out = operate(slopes, y_pair, z_pair, gain)
            else:
                arrived = [across(crossed, t * sublanes + r) for r in each]
                firsts = [
                    slope[0, t, r] * (1 / 6) + value * 0.125 + tiled(product, t, r) * (1 / 24)
                    for r, value in zip(each, arrived)
                ]
                seconds = [
                    slope[0, t, r] * 0.5 + across(crossed, t * sublanes + r) * (1 / 6) + value
                    for r, value in zip(each, operate(firsts, y_pair, z_pair, gain))
                ]
                out = [
                    0.5 * (slope[0, t, r] + tiled(state, t, r)) + value
                    for r, value in zip(each, operate(seconds, y_pair, z_pair, gain))
                ]
            for r, value in zip(each, out):
                result_ref[0, inner * tiles + t, pl.ds(r, grid_y, stride=sublanes), :] = value
        return carry

    lax.fori_loop(0, tiles, per_tile, 0, unroll=tiles if stage == "first" else 1)
    if stage == "first":
        return

    @pl.when(inner == pl.num_programs(1) - 1)
    def _():
        owners, _, columns = sent_ref.shape[:3]

        def per_owner(d, carry):
            for c in range(columns):
                start = pl.multiple_of((d * columns + c) * sublanes, sublanes)
                block = result_ref[0, :, pl.ds(start, sublanes), :].reshape(lanes, lanes)
                sent_ref[d, 0, c] = block.T
            return carry

        lax.fori_loop(0, owners, per_owner, 0)


def stage_call(stage, harmonic, groups, grid_y, width, y_operator, z_operator, gain, *operands):
    chunk = tiles * sublanes
    inner = lanes // chunk
    per = width // lanes
    row_tiles = width // sublanes
    rows = grid_y * sublanes

    def whole(shape):
        return pl.BlockSpec((1, *shape), lambda k, i: (harmonic, 0, 0))

    def tile_spec(which):
        return pl.BlockSpec((1, tiles, rows, lanes), lambda k, i: (which, k * inner + i, 0, 0))

    by_rows = pl.BlockSpec((groups, 1, per, chunk, lanes), lambda k, i: (0, k, 0, i, 0))
    unturned = pl.BlockSpec((groups, per, 1, lanes, lanes), lambda k, i: (0, 0, k, 0, 0))
    turned = pl.BlockSpec((grid_y, chunk, lanes), lambda k, i: (0, k * inner + i, 0))
    slope = pl.BlockSpec(
        (1, tiles, sublanes, grid_y, lanes), lambda k, i: (0, k * inner + i, 0, 0, 0)
    )
    ins = {
        "first": [tile_spec(harmonic)],
        "second": [unturned, by_rows, tile_spec(harmonic)],
        "third": [turned, tile_spec(0), slope, tile_spec(harmonic)],
    }[stage]
    blocks = jax.ShapeDtypeStruct((groups, per, per, lanes, lanes), jnp.float32)
    if stage == "first":
        out_specs, out_shape = [by_rows], [blocks]
    else:
        out_specs = [
            pl.BlockSpec((1, lanes // sublanes, rows, lanes), lambda k, i: (0, k, 0, 0)),
            pl.BlockSpec((groups, 1, per, lanes, lanes), lambda k, i: (0, k, 0, 0, 0)),
        ]
        out_shape = [jax.ShapeDtypeStruct((1, row_tiles, rows, lanes), jnp.float32), blocks]
    scratch = [
        pltpu.VMEM((2 * grid_y, 2 * grid_y), jnp.bfloat16),
        pltpu.VMEM((2 * lanes, 2 * lanes), jnp.bfloat16),
    ]
    if stage == "second":
        out_specs.append(slope)
        out_shape.append(
            jax.ShapeDtypeStruct((1, row_tiles, sublanes, grid_y, lanes), jnp.float32)
        )
        scratch.insert(0, pltpu.VMEM((grid_y, lanes, lanes), jnp.float32))
    if stage == "first":
        scratch.insert(0, pltpu.VMEM((tiles, rows, lanes), jnp.float32))
    passes = 2 if stage == "third" else 1
    return pl.pallas_call(
        functools.partial(body, stage, grid_y),
        grid=(per, inner),
        in_specs=[
            whole((grid_y, grid_y)),
            whole((lanes, lanes)),
            whole((grid_y, lanes)),
            *ins,
        ],
        out_specs=out_specs,
        out_shape=out_shape,
        scratch_shapes=scratch,
        cost_estimate=pl.CostEstimate(
            flops=passes * 16 * width * grid_y * lanes * (grid_y + lanes),
            bytes_accessed=(len(ins) + len(out_specs)) * width * grid_y * lanes * 4,
            transcendentals=0,
        ),
        compiler_params=pltpu.CompilerParams(vmem_limit_bytes=60 * 1024 * 1024),
        name=f"{stage}_{harmonic}",
    )(y_operator, z_operator, gain, *operands)


def finish_body(*refs):
    product_ref, crossed_ref, out_ref = refs[0], refs[1], refs[-1]
    for y in range(crossed_ref.shape[0]):
        part = product_ref[0, :, y * sublanes : (y + 1) * sublanes, :]
        out_ref[0, :, y * lanes : (y + 1) * lanes] = part.reshape(-1, lanes) + crossed_ref[y]


def finish_call(harmonic, product, crossed, out):
    grid_y, width, _ = crossed.shape
    row_tiles = lanes // sublanes // 2
    chunk = row_tiles * sublanes
    in_specs = [
        pl.BlockSpec((1, row_tiles, grid_y * sublanes, lanes), lambda i: (0, i, 0, 0)),
        pl.BlockSpec((grid_y, chunk, lanes), lambda i: (0, i, 0)),
    ]
    operands = [product, crossed]
    aliases = {}
    if out is not None:
        in_specs.append(pl.BlockSpec(memory_space=pl.ANY))
        operands.append(out)
        aliases = {2: 0}
    return pl.pallas_call(
        finish_body,
        grid=(width // chunk,),
        in_specs=in_specs,
        out_specs=pl.BlockSpec((1, chunk, grid_y * lanes), lambda i: (harmonic, i, 0)),
        out_shape=jax.ShapeDtypeStruct((2, width, grid_y * lanes), jnp.float32),
        input_output_aliases=aliases,
        cost_estimate=pl.CostEstimate(
            flops=width * grid_y * lanes,
            bytes_accessed=3 * width * grid_y * lanes * 4,
            transcendentals=0,
        ),
        compiler_params=pltpu.CompilerParams(vmem_limit_bytes=60 * 1024 * 1024),
        name=f"finish_{harmonic}",
    )(*operands)


def exchange(sent):
    return lax.all_to_all(sent, "col", split_axis=0, concat_axis=0, tiled=True)


def on_device_tiled(covariance, forcing, coefficient, y_operator, z_operator):
    groups = lax.axis_size("col")
    width = covariance.shape[1]
    per = width // lanes
    grid_y = y_operator.shape[1]

    def by_tiles(value):
        cut = value.reshape(2, width // sublanes, sublanes, grid_y, lanes)
        return jnp.swapaxes(cut, 2, 3).reshape(2, width // sublanes, grid_y * sublanes, lanes)

    def by_y(blocks):
        return blocks.reshape(groups * per, per * lanes, lanes)

    state, source = by_tiles(covariance), by_tiles(forcing)

    def call(stage, harmonic, *operands):
        return stage_call(
            stage, harmonic, groups, grid_y, width, y_operator, z_operator, coefficient, *operands
        )

    first = [call("first", h, state)[0] for h in range(2)]
    crossed = [exchange(sent) for sent in first]
    second = [call("second", h, crossed[h], first[h], source) for h in range(2)]
    crossed = [by_y(exchange(sent)) for _, sent, _ in second]
    third = [call("third", h, crossed[h], second[h][0], second[h][2], state) for h in range(2)]
    crossed = [by_y(exchange(sent)) for _, sent in third]
    out = None
    for h in range(2):
        out = finish_call(h, third[h][0], crossed[h], out)
    return out


def on_device_plain(covariance, forcing, coefficient, y_operator, z_operator):
    grid_y, grid_z = y_operator.shape[1], z_operator.shape[1]
    width = covariance.shape[1]
    groups = lax.axis_size("col")

    def along(values):
        part = jnp.einsum("hya,hcaz->hcyz", y_operator, values, precision=lax.Precision.HIGHEST)
        other = jnp.einsum("hcyb,hzb->hcyz", values, z_operator, precision=lax.Precision.HIGHEST)
        return part + other

    def operated(slab):
        grid = slab.reshape(2, width, grid_y, grid_z)
        return along(step_size * coefficient[:, None] * along(grid)).reshape(slab.shape)

    def crossed(product):
        received = lax.all_to_all(product, "col", split_axis=2, concat_axis=2, tiled=True)
        blocks = received.reshape(2, width, groups, width)
        return jnp.swapaxes(blocks, 1, 3).reshape(2, width, groups * width)

    product = operated(covariance)
    slope = product + crossed(product) + step_size * forcing
    product = operated(slope)
    other = crossed(product)
    inner = slope / 2 + other / 6 + operated(slope / 6 + other / 8 + product / 24)
    half = (covariance + slope) / 2 + operated(inner)
    return half + crossed(half)


def on_device(covariance, forcing, coefficient, y_operator, z_operator):
    width = covariance.shape[1]
    grid_y, grid_z = y_operator.shape[1], z_operator.shape[1]
    tiled = grid_z == lanes and width % lanes == 0 and grid_y % 16 == 0
    chosen = on_device_tiled if tiled else on_device_plain
    return chosen(covariance, forcing, coefficient, y_operator, z_operator)


def solution(mesh):
    placed = (P(None, "col", None), P(None, "col", None), P(), P(), P())
    return jax.shard_map(
        on_device, mesh=mesh, in_specs=placed, out_specs=P(None, "col", None), check_vma=False
    )
```

```python
import functools

import jax
import jax.numpy as jnp
from jax import lax
from jax.experimental import pallas as pl
from jax.experimental.pallas import tpu as pltpu
from jax.sharding import PartitionSpec as P

step_size = 0.2
lanes = 128
sublanes = 8
tiles = 8
group = sublanes


def split(value):
    high = value.astype(jnp.bfloat16)
    low = (value - high.astype(jnp.float32)).astype(jnp.bfloat16)
    return high, low


def combined(rows, y_pair, z_pair):
    grid_y = rows[0].shape[0]
    pairs = [split(row) for row in rows]
    right = jnp.concatenate([jnp.concatenate(pair, axis=0) for pair in pairs], axis=1)
    left = jnp.concatenate([jnp.concatenate(pair, axis=1) for pair in pairs], axis=0)
    along_y = jnp.dot(y_pair, right, preferred_element_type=jnp.float32)
    along_z = jnp.dot(left, z_pair, preferred_element_type=jnp.float32)
    out = []
    for i in range(len(rows)):
        y_part = along_y[:, i * lanes : (i + 1) * lanes]
        z_part = along_z[i * grid_y : (i + 1) * grid_y]
        out.append(
            (y_part[:grid_y] + y_part[grid_y:]) + (z_part[:, :lanes] + z_part[:, lanes:])
        )
    return out


def operate(rows, y_pair, z_pair, gain):
    inner = [gain * row for row in combined(rows, y_pair, z_pair)]
    return combined(inner, y_pair, z_pair)


def prepare(y_ref, z_ref, y_pair_ref, z_pair_ref):
    grid_y = y_ref.shape[1]
    for part, value in enumerate(split(y_ref[0])):
        for side in range(2):
            y_pair_ref[pl.ds(part * grid_y, grid_y), pl.ds(side * grid_y, grid_y)] = value
    for part, value in enumerate(split(z_ref[0].T)):
        for side in range(2):
            z_pair_ref[pl.ds(side * lanes, lanes), pl.ds(part * lanes, lanes)] = value


def body(stage, grid_y, *refs):
    y_ref, z_ref, gain_ref, *refs = refs
    *refs, y_pair_ref, z_pair_ref = refs
    half, inner = pl.program_id(0), pl.program_id(1)
    chunk = tiles * sublanes

    @pl.when((half == 0) & (inner == 0))
    def _():
        prepare(y_ref, z_ref, y_pair_ref, z_pair_ref)

    if stage == "first":
        state, sent_ref = refs
    elif stage == "second":
        crossed, product, forcing, result_ref, sent_ref, slope_ref, turned_ref = refs
        owners, per = crossed.shape[:2]

        @pl.when(inner == 0)
        def _():
            def per_source(s, carry):
                for k in range(per):
                    turned_ref[s * per + k] = crossed[s, k, 0].T
                return carry

            lax.fori_loop(0, owners, per_source, 0)

    else:
        crossed, product, slope, state, result_ref, sent_ref = refs
    y_pair, z_pair, gain = y_pair_ref[...], z_pair_ref[...], step_size * gain_ref[0]

    def tiled(ref, t, r):
        return ref[0, t, pl.ds(r, grid_y, stride=sublanes), :]

    def across(ref, row):
        rows = ref.shape[-2]
        return ref.reshape(grid_y * rows, lanes)[pl.ds(row, grid_y, stride=rows), :]

    def per_tile(t, carry):
        for r0 in range(0, sublanes, group):
            each = range(r0, r0 + group)
            if stage == "first":
                out = operate([tiled(state, t, r) for r in each], y_pair, z_pair, gain)
                flat = sent_ref.reshape(grid_y * chunk, lanes)
                for j in range(0, grid_y, sublanes):
                    cube = jnp.stack([value[j : j + sublanes] for value in out])
                    cube = jnp.swapaxes(cube, 0, 1)
                    for y in range(sublanes):
                        start = pl.multiple_of((j + y) * chunk + t * sublanes, sublanes)
                        flat[pl.ds(start, sublanes), :] = cube[y]
                continue
            if stage == "second":
                slopes = [
                    across(product, t * sublanes + r)
                    + across(turned_ref, inner * chunk + t * sublanes + r)
                    + step_size * tiled(forcing, t, r)
                    for r in each
                ]
                for r, value in zip(each, slopes):
                    slope_ref[0, t, r] = value
                out = operate(slopes, y_pair, z_pair, gain)
            else:
                arrived = [across(crossed, t * sublanes + r) for r in each]
                firsts = [
                    slope[0, t, r] * (1 / 6) + value * 0.125 + tiled(product, t, r) * (1 / 24)
                    for r, value in zip(each, arrived)
                ]
                seconds = [
                    slope[0, t, r] * 0.5 + across(crossed, t * sublanes + r) * (1 / 6) + value
                    for r, value in zip(each, operate(firsts, y_pair, z_pair, gain))
                ]
                out = [
                    0.5 * (slope[0, t, r] + tiled(state, t, r)) + value
                    for r, value in zip(each, operate(seconds, y_pair, z_pair, gain))
                ]
            for r, value in zip(each, out):
                result_ref[0, inner * tiles + t, pl.ds(r, grid_y, stride=sublanes), :] = value
        return carry

    lax.fori_loop(0, tiles, per_tile, 0, unroll=tiles if stage == "first" else 1)
    if stage == "first":
        return

    @pl.when(inner == pl.num_programs(1) - 1)
    def _():
        owners, _, columns = sent_ref.shape[:3]

        def per_owner(d, carry):
            for c in range(columns):
                start = pl.multiple_of((d * columns + c) * sublanes, sublanes)
                block = result_ref[0, :, pl.ds(start, sublanes), :].reshape(lanes, lanes)
                sent_ref[d, 0, c] = block.T
            return carry

        lax.fori_loop(0, owners, per_owner, 0)


def stage_call(stage, harmonic, groups, grid_y, width, y_operator, z_operator, gain, *operands):
    chunk = tiles * sublanes
    inner = lanes // chunk
    per = width // lanes
    row_tiles = width // sublanes
    rows = grid_y * sublanes

    def whole(shape):
        return pl.BlockSpec((1, *shape), lambda k, i: (harmonic, 0, 0))

    def tile_spec(which):
        return pl.BlockSpec((1, tiles, rows, lanes), lambda k, i: (which, k * inner + i, 0, 0))

    by_rows = pl.BlockSpec((groups, 1, per, chunk, lanes), lambda k, i: (0, k, 0, i, 0))
    unturned = pl.BlockSpec((groups, per, 1, lanes, lanes), lambda k, i: (0, 0, k, 0, 0))
    turned = pl.BlockSpec((grid_y, chunk, lanes), lambda k, i: (0, k * inner + i, 0))
    slope = pl.BlockSpec(
        (1, tiles, sublanes, grid_y, lanes), lambda k, i: (0, k * inner + i, 0, 0, 0)
    )
    ins = {
        "first": [tile_spec(harmonic)],
        "second": [unturned, by_rows, tile_spec(harmonic)],
        "third": [turned, tile_spec(0), slope, tile_spec(harmonic)],
    }[stage]
    blocks = jax.ShapeDtypeStruct((groups, per, per, lanes, lanes), jnp.float32)
    if stage == "first":
        out_specs, out_shape = [by_rows], [blocks]
    else:
        out_specs = [
            pl.BlockSpec((1, lanes // sublanes, rows, lanes), lambda k, i: (0, k, 0, 0)),
            pl.BlockSpec((groups, 1, per, lanes, lanes), lambda k, i: (0, k, 0, 0, 0)),
        ]
        out_shape = [jax.ShapeDtypeStruct((1, row_tiles, rows, lanes), jnp.float32), blocks]
    scratch = [
        pltpu.VMEM((2 * grid_y, 2 * grid_y), jnp.bfloat16),
        pltpu.VMEM((2 * lanes, 2 * lanes), jnp.bfloat16),
    ]
    if stage == "second":
        out_specs.append(slope)
        out_shape.append(
            jax.ShapeDtypeStruct((1, row_tiles, sublanes, grid_y, lanes), jnp.float32)
        )
        scratch.insert(0, pltpu.VMEM((grid_y, lanes, lanes), jnp.float32))
    passes = 2 if stage == "third" else 1
    return pl.pallas_call(
        functools.partial(body, stage, grid_y),
        grid=(per, inner),
        in_specs=[
            whole((grid_y, grid_y)),
            whole((lanes, lanes)),
            whole((grid_y, lanes)),
            *ins,
        ],
        out_specs=out_specs,
        out_shape=out_shape,
        scratch_shapes=scratch,
        cost_estimate=pl.CostEstimate(
            flops=passes * 16 * width * grid_y * lanes * (grid_y + lanes),
            bytes_accessed=(len(ins) + len(out_specs)) * width * grid_y * lanes * 4,
            transcendentals=0,
        ),
        compiler_params=pltpu.CompilerParams(vmem_limit_bytes=60 * 1024 * 1024),
        name=f"{stage}_{harmonic}",
    )(y_operator, z_operator, gain, *operands)


def finish_body(*refs):
    product_ref, crossed_ref, out_ref = refs[0], refs[1], refs[-1]
    for y in range(crossed_ref.shape[0]):
        part = product_ref[0, :, y * sublanes : (y + 1) * sublanes, :]
        out_ref[0, :, y * lanes : (y + 1) * lanes] = part.reshape(-1, lanes) + crossed_ref[y]


def finish_call(harmonic, product, crossed, out):
    grid_y, width, _ = crossed.shape
    row_tiles = lanes // sublanes // 2
    chunk = row_tiles * sublanes
    in_specs = [
        pl.BlockSpec((1, row_tiles, grid_y * sublanes, lanes), lambda i: (0, i, 0, 0)),
        pl.BlockSpec((grid_y, chunk, lanes), lambda i: (0, i, 0)),
    ]
    operands = [product, crossed]
    aliases = {}
    if out is not None:
        in_specs.append(pl.BlockSpec(memory_space=pl.ANY))
        operands.append(out)
        aliases = {2: 0}
    return pl.pallas_call(
        finish_body,
        grid=(width // chunk,),
        in_specs=in_specs,
        out_specs=pl.BlockSpec((1, chunk, grid_y * lanes), lambda i: (harmonic, i, 0)),
        out_shape=jax.ShapeDtypeStruct((2, width, grid_y * lanes), jnp.float32),
        input_output_aliases=aliases,
        cost_estimate=pl.CostEstimate(
            flops=width * grid_y * lanes,
            bytes_accessed=3 * width * grid_y * lanes * 4,
            transcendentals=0,
        ),
        compiler_params=pltpu.CompilerParams(vmem_limit_bytes=60 * 1024 * 1024),
        name=f"finish_{harmonic}",
    )(*operands)


def exchange(sent):
    return lax.all_to_all(sent, "col", split_axis=0, concat_axis=0, tiled=True)


def on_device_tiled(covariance, forcing, coefficient, y_operator, z_operator):
    groups = lax.axis_size("col")
    width = covariance.shape[1]
    per = width // lanes
    grid_y = y_operator.shape[1]

    def by_tiles(value):
        cut = value.reshape(2, width // sublanes, sublanes, grid_y, lanes)
        return jnp.swapaxes(cut, 2, 3).reshape(2, width // sublanes, grid_y * sublanes, lanes)

    def by_y(blocks):
        return blocks.reshape(groups * per, per * lanes, lanes)

    state, source = by_tiles(covariance), by_tiles(forcing)

    def call(stage, harmonic, *operands):
        return stage_call(
            stage, harmonic, groups, grid_y, width, y_operator, z_operator, coefficient, *operands
        )

    first = [call("first", h, state)[0] for h in range(2)]
    crossed = [exchange(sent) for sent in first]
    second = [call("second", h, crossed[h], first[h], source) for h in range(2)]
    crossed = [by_y(exchange(sent)) for _, sent, _ in second]
    third = [call("third", h, crossed[h], second[h][0], second[h][2], state) for h in range(2)]
    crossed = [by_y(exchange(sent)) for _, sent in third]
    out = None
    for h in range(2):
        out = finish_call(h, third[h][0], crossed[h], out)
    return out


def on_device_plain(covariance, forcing, coefficient, y_operator, z_operator):
    grid_y, grid_z = y_operator.shape[1], z_operator.shape[1]
    width = covariance.shape[1]
    groups = lax.axis_size("col")

    def along(values):
        part = jnp.einsum("hya,hcaz->hcyz", y_operator, values, precision=lax.Precision.HIGHEST)
        other = jnp.einsum("hcyb,hzb->hcyz", values, z_operator, precision=lax.Precision.HIGHEST)
        return part + other

    def operated(slab):
        grid = slab.reshape(2, width, grid_y, grid_z)
        return along(step_size * coefficient[:, None] * along(grid)).reshape(slab.shape)

    def crossed(product):
        received = lax.all_to_all(product, "col", split_axis=2, concat_axis=2, tiled=True)
        blocks = received.reshape(2, width, groups, width)
        return jnp.swapaxes(blocks, 1, 3).reshape(2, width, groups * width)

    product = operated(covariance)
    slope = product + crossed(product) + step_size * forcing
    product = operated(slope)
    other = crossed(product)
    inner = slope / 2 + other / 6 + operated(slope / 6 + other / 8 + product / 24)
    half = (covariance + slope) / 2 + operated(inner)
    return half + crossed(half)


def on_device(covariance, forcing, coefficient, y_operator, z_operator):
    width = covariance.shape[1]
    grid_y, grid_z = y_operator.shape[1], z_operator.shape[1]
    tiled = grid_z == lanes and width % lanes == 0 and grid_y % 16 == 0
    chosen = on_device_tiled if tiled else on_device_plain
    return chosen(covariance, forcing, coefficient, y_operator, z_operator)


def solution(mesh):
    placed = (P(None, "col", None), P(None, "col", None), P(), P(), P())
    return jax.shard_map(
        on_device, mesh=mesh, in_specs=placed, out_specs=P(None, "col", None), check_vma=False
    )
```

```python
import functools

import jax
import jax.numpy as jnp
from jax import lax
from jax.experimental import pallas as pl
from jax.experimental.pallas import tpu as pltpu
from jax.sharding import PartitionSpec as P

step_size = 0.2
lanes = 128
sublanes = 8
tiles = 8
group = sublanes


def split(value):
    high = value.astype(jnp.bfloat16)
    low = (value - high.astype(jnp.float32)).astype(jnp.bfloat16)
    return high, low


def combined(rows, y_pair, z_pair):
    grid_y = rows[0].shape[0]
    pairs = [split(row) for row in rows]
    right = jnp.concatenate([jnp.concatenate(pair, axis=0) for pair in pairs], axis=1)
    left = jnp.concatenate([jnp.concatenate(pair, axis=1) for pair in pairs], axis=0)
    along_y = jnp.dot(y_pair, right, preferred_element_type=jnp.float32)
    along_z = jnp.dot(left, z_pair, preferred_element_type=jnp.float32)
    out = []
    for i in range(len(rows)):
        y_part = along_y[:, i * lanes : (i + 1) * lanes]
        z_part = along_z[i * grid_y : (i + 1) * grid_y]
        out.append(
            (y_part[:grid_y] + y_part[grid_y:]) + (z_part[:, :lanes] + z_part[:, lanes:])
        )
    return out


def operate(rows, y_pair, z_pair, gain):
    inner = [row * gain for row in combined(rows, y_pair, z_pair)]
    return combined(inner, y_pair, z_pair)


def prepare(y_ref, z_ref, y_pair_ref, z_pair_ref):
    grid_y = y_ref.shape[1]
    for part, value in enumerate(split(y_ref[0])):
        for side in range(2):
            y_pair_ref[pl.ds(part * grid_y, grid_y), pl.ds(side * grid_y, grid_y)] = value
    for part, value in enumerate(split(z_ref[0].T)):
        for side in range(2):
            z_pair_ref[pl.ds(side * lanes, lanes), pl.ds(part * lanes, lanes)] = value


def body(stage, grid_y, *refs):
    y_ref, z_ref, gain_ref, *refs = refs
    *refs, y_pair_ref, z_pair_ref = refs
    half, inner = pl.program_id(0), pl.program_id(1)
    chunk = tiles * sublanes

    @pl.when((half == 0) & (inner == 0))
    def _():
        prepare(y_ref, z_ref, y_pair_ref, z_pair_ref)

    if stage == "first":
        state, sent_ref = refs
    elif stage == "second":
        crossed, product, forcing, result_ref, sent_ref, slope_ref, turned_ref = refs
        owners, per = crossed.shape[:2]

        @pl.when(inner == 0)
        def _():
            def per_source(s, carry):
                for k in range(per):
                    turned_ref[s * per + k] = crossed[s, k, 0].T
                return carry

            lax.fori_loop(0, owners, per_source, 0)

    else:
        crossed, product, slope, state, result_ref, sent_ref = refs
    y_pair, z_pair, gain = y_pair_ref[...], z_pair_ref[...], step_size * gain_ref[0]

    def tiled(ref, t, r):
        return ref[0, t, pl.ds(r, grid_y, stride=sublanes), :]

    def across(ref, row):
        rows = ref.shape[-2]
        return ref.reshape(grid_y * rows, lanes)[pl.ds(row, grid_y, stride=rows), :]

    def per_tile(t, carry):
        for r0 in range(0, sublanes, group):
            each = range(r0, r0 + group)
            if stage == "first":
                out = operate([tiled(state, t, r) for r in each], y_pair, z_pair, gain)
                flat = sent_ref.reshape(grid_y * chunk, lanes)
                for j in range(0, grid_y, sublanes):
                    cube = jnp.stack([value[j : j + sublanes] for value in out])
                    cube = jnp.swapaxes(cube, 0, 1)
                    for y in range(sublanes):
                        start = pl.multiple_of((j + y) * chunk + t * sublanes, sublanes)
                        flat[pl.ds(start, sublanes), :] = cube[y]
                continue
            if stage == "second":
                slopes = [
                    across(product, t * sublanes + r)
                    + across(turned_ref, inner * chunk + t * sublanes + r)
                    + step_size * tiled(forcing, t, r)
                    for r in each
                ]
                for r, value in zip(each, slopes):
                    slope_ref[0, t, r] = value
                out = operate(slopes, y_pair, z_pair, gain)
            else:
                arrived = [across(crossed, t * sublanes + r) for r in each]
                firsts = [
                    slope[0, t, r] * (1 / 6) + value * 0.125 + tiled(product, t, r) * (1 / 24)
                    for r, value in zip(each, arrived)
                ]
                seconds = [
                    slope[0, t, r] * 0.5 + across(crossed, t * sublanes + r) * (1 / 6) + value
                    for r, value in zip(each, operate(firsts, y_pair, z_pair, gain))
                ]
                out = [
                    0.5 * (slope[0, t, r] + tiled(state, t, r)) + value
                    for r, value in zip(each, operate(seconds, y_pair, z_pair, gain))
                ]
            for r, value in zip(each, out):
                result_ref[0, inner * tiles + t, pl.ds(r, grid_y, stride=sublanes), :] = value
        return carry

    lax.fori_loop(0, tiles, per_tile, 0, unroll=tiles if stage == "first" else 1)
    if stage == "first":
        return

    @pl.when(inner == pl.num_programs(1) - 1)
    def _():
        owners, _, columns = sent_ref.shape[:3]

        def per_owner(d, carry):
            for c in range(columns):
                start = pl.multiple_of((d * columns + c) * sublanes, sublanes)
                block = result_ref[0, :, pl.ds(start, sublanes), :].reshape(lanes, lanes)
                sent_ref[d, 0, c] = block.T
            return carry

        lax.fori_loop(0, owners, per_owner, 0)


def stage_call(stage, harmonic, groups, grid_y, width, y_operator, z_operator, gain, *operands):
    chunk = tiles * sublanes
    inner = lanes // chunk
    per = width // lanes
    row_tiles = width // sublanes
    rows = grid_y * sublanes

    def whole(shape):
        return pl.BlockSpec((1, *shape), lambda k, i: (harmonic, 0, 0))

    def tile_spec(which):
        return pl.BlockSpec((1, tiles, rows, lanes), lambda k, i: (which, k * inner + i, 0, 0))

    by_rows = pl.BlockSpec((groups, 1, per, chunk, lanes), lambda k, i: (0, k, 0, i, 0))
    unturned = pl.BlockSpec((groups, per, 1, lanes, lanes), lambda k, i: (0, 0, k, 0, 0))
    turned = pl.BlockSpec((grid_y, chunk, lanes), lambda k, i: (0, k * inner + i, 0))
    slope = pl.BlockSpec(
        (1, tiles, sublanes, grid_y, lanes), lambda k, i: (0, k * inner + i, 0, 0, 0)
    )
    ins = {
        "first": [tile_spec(harmonic)],
        "second": [unturned, by_rows, tile_spec(harmonic)],
        "third": [turned, tile_spec(0), slope, tile_spec(harmonic)],
    }[stage]
    blocks = jax.ShapeDtypeStruct((groups, per, per, lanes, lanes), jnp.float32)
    if stage == "first":
        out_specs, out_shape = [by_rows], [blocks]
    else:
        out_specs = [
            pl.BlockSpec((1, lanes // sublanes, rows, lanes), lambda k, i: (0, k, 0, 0)),
            pl.BlockSpec((groups, 1, per, lanes, lanes), lambda k, i: (0, k, 0, 0, 0)),
        ]
        out_shape = [jax.ShapeDtypeStruct((1, row_tiles, rows, lanes), jnp.float32), blocks]
    scratch = [
        pltpu.VMEM((2 * grid_y, 2 * grid_y), jnp.bfloat16),
        pltpu.VMEM((2 * lanes, 2 * lanes), jnp.bfloat16),
    ]
    if stage == "second":
        out_specs.append(slope)
        out_shape.append(
            jax.ShapeDtypeStruct((1, row_tiles, sublanes, grid_y, lanes), jnp.float32)
        )
        scratch.insert(0, pltpu.VMEM((grid_y, lanes, lanes), jnp.float32))
    passes = 2 if stage == "third" else 1
    return pl.pallas_call(
        functools.partial(body, stage, grid_y),
        grid=(per, inner),
        in_specs=[
            whole((grid_y, grid_y)),
            whole((lanes, lanes)),
            whole((grid_y, lanes)),
            *ins,
        ],
        out_specs=out_specs,
        out_shape=out_shape,
        scratch_shapes=scratch,
        cost_estimate=pl.CostEstimate(
            flops=passes * 16 * width * grid_y * lanes * (grid_y + lanes),
            bytes_accessed=(len(ins) + len(out_specs)) * width * grid_y * lanes * 4,
            transcendentals=0,
        ),
        compiler_params=pltpu.CompilerParams(vmem_limit_bytes=60 * 1024 * 1024),
        name=f"{stage}_{harmonic}",
    )(y_operator, z_operator, gain, *operands)


def finish_body(*refs):
    product_ref, crossed_ref, out_ref = refs[0], refs[1], refs[-1]
    for y in range(crossed_ref.shape[0]):
        part = product_ref[0, :, y * sublanes : (y + 1) * sublanes, :]
        out_ref[0, :, y * lanes : (y + 1) * lanes] = part.reshape(-1, lanes) + crossed_ref[y]


def finish_call(harmonic, product, crossed, out):
    grid_y, width, _ = crossed.shape
    row_tiles = lanes // sublanes // 2
    chunk = row_tiles * sublanes
    in_specs = [
        pl.BlockSpec((1, row_tiles, grid_y * sublanes, lanes), lambda i: (0, i, 0, 0)),
        pl.BlockSpec((grid_y, chunk, lanes), lambda i: (0, i, 0)),
    ]
    operands = [product, crossed]
    aliases = {}
    if out is not None:
        in_specs.append(pl.BlockSpec(memory_space=pl.ANY))
        operands.append(out)
        aliases = {2: 0}
    return pl.pallas_call(
        finish_body,
        grid=(width // chunk,),
        in_specs=in_specs,
        out_specs=pl.BlockSpec((1, chunk, grid_y * lanes), lambda i: (harmonic, i, 0)),
        out_shape=jax.ShapeDtypeStruct((2, width, grid_y * lanes), jnp.float32),
        input_output_aliases=aliases,
        cost_estimate=pl.CostEstimate(
            flops=width * grid_y * lanes,
            bytes_accessed=3 * width * grid_y * lanes * 4,
            transcendentals=0,
        ),
        compiler_params=pltpu.CompilerParams(vmem_limit_bytes=60 * 1024 * 1024),
        name=f"finish_{harmonic}",
    )(*operands)


def exchange(sent):
    return lax.all_to_all(sent, "col", split_axis=0, concat_axis=0, tiled=True)


def on_device_tiled(covariance, forcing, coefficient, y_operator, z_operator):
    groups = lax.axis_size("col")
    width = covariance.shape[1]
    per = width // lanes
    grid_y = y_operator.shape[1]

    def by_tiles(value):
        cut = value.reshape(2, width // sublanes, sublanes, grid_y, lanes)
        return jnp.swapaxes(cut, 2, 3).reshape(2, width // sublanes, grid_y * sublanes, lanes)

    def by_y(blocks):
        return blocks.reshape(groups * per, per * lanes, lanes)

    state, source = by_tiles(covariance), by_tiles(forcing)

    def call(stage, harmonic, *operands):
        return stage_call(
            stage, harmonic, groups, grid_y, width, y_operator, z_operator, coefficient, *operands
        )

    first = [call("first", h, state)[0] for h in range(2)]
    crossed = [exchange(sent) for sent in first]
    second = [call("second", h, crossed[h], first[h], source) for h in range(2)]
    crossed = [by_y(exchange(sent)) for _, sent, _ in second]
    third = [call("third", h, crossed[h], second[h][0], second[h][2], state) for h in range(2)]
    crossed = [by_y(exchange(sent)) for _, sent in third]
    out = None
    for h in range(2):
        out = finish_call(h, third[h][0], crossed[h], out)
    return out


def on_device_plain(covariance, forcing, coefficient, y_operator, z_operator):
    grid_y, grid_z = y_operator.shape[1], z_operator.shape[1]
    width = covariance.shape[1]
    groups = lax.axis_size("col")

    def along(values):
        part = jnp.einsum("hya,hcaz->hcyz", y_operator, values, precision=lax.Precision.HIGHEST)
        other = jnp.einsum("hcyb,hzb->hcyz", values, z_operator, precision=lax.Precision.HIGHEST)
        return part + other

    def operated(slab):
        grid = slab.reshape(2, width, grid_y, grid_z)
        return along(step_size * coefficient[:, None] * along(grid)).reshape(slab.shape)

    def crossed(product):
        received = lax.all_to_all(product, "col", split_axis=2, concat_axis=2, tiled=True)
        blocks = received.reshape(2, width, groups, width)
        return jnp.swapaxes(blocks, 1, 3).reshape(2, width, groups * width)

    product = operated(covariance)
    slope = product + crossed(product) + step_size * forcing
    product = operated(slope)
    other = crossed(product)
    inner = slope / 2 + other / 6 + operated(slope / 6 + other / 8 + product / 24)
    half = (covariance + slope) / 2 + operated(inner)
    return half + crossed(half)


def on_device(covariance, forcing, coefficient, y_operator, z_operator):
    width = covariance.shape[1]
    grid_y, grid_z = y_operator.shape[1], z_operator.shape[1]
    tiled = grid_z == lanes and width % lanes == 0 and grid_y % 16 == 0
    chosen = on_device_tiled if tiled else on_device_plain
    return chosen(covariance, forcing, coefficient, y_operator, z_operator)


def solution(mesh):
    placed = (P(None, "col", None), P(None, "col", None), P(), P(), P())
    return jax.shard_map(
        on_device, mesh=mesh, in_specs=placed, out_specs=P(None, "col", None), check_vma=False
    )
```
